32 devices in a mesh: dp: 4 (over y, x), vocab: 8 (over z, core).
Axes of the slice: x: 2, y: 2, z: 4, core: 2. Of those that a mesh axis runs over, the one named last changes fastest.
Arguments:
- hidden: bfloat16 [1024, 5120], P('dp')
- head_t: bfloat16 [5120, 19456], P('dp', 'vocab'), may hold values from -0.25 to 0.25
- targets: int32 [1024], P('dp'), may hold values from 0 to 19455
- token_ids: int32 [1024], P('dp'), may hold values from 0 to 19455, as said below
- embed_cot: bfloat16 [1024, 5120], P('dp'), may hold values from -6 to 6
Outputs:
- head_grad: bfloat16 [5120, 19456], P('dp', 'vocab')
- embed_grad: bfloat16 [5120, 19456], P('dp', 'vocab')
- hidden_grad: bfloat16 [1024, 5120], P('vocab', 'dp')
The draws below stay inside these ranges and needn't reach their ends.
Inputs may be any that keep to these rules, and one draw needn't show every extreme that they name: `token_ids`: among the 256 input ids of one data group, at most 64 lie in any one block of 2432 vocabulary rows that starts at a multiple of 2432; in every group some block holds exactly 64.
All inputs are finite; a program needn't handle non-finite values.
Results may differ from the reference program's by a relative error of at most 0.0033.
Values may be sent and summed in bfloat16 or wider, within the bound.
A program may use at most 128 MiB of HBM per device.

```python
import math
import jax
import jax.numpy as jnp
import numpy as np

D = 5120
V_DEV = 2432
TOK_DEV = 256
VOCAB = 19456
TOKENS = 1024


def draw_hidden(key, part):
    base_key = jax.random.fold_in(key, 11)
    values = jax.random.normal(base_key, (TOKENS, D), jnp.float32)
    strong_rows = jax.random.randint(jax.random.fold_in(key, 13), (4,), 0, TOKENS)
    strengths = jnp.array([20.0, 30.0, 40.0, 45.0], jnp.float32)
    row_numbers = jnp.arange(TOKENS, dtype=jnp.int32)
    boost = jnp.ones((TOKENS,), jnp.float32)
    boost = jnp.where(row_numbers == strong_rows[0], strengths[0], boost)
    boost = jnp.where(row_numbers == strong_rows[1], strengths[1], boost)
    boost = jnp.where(row_numbers == strong_rows[2], strengths[2], boost)
    boost = jnp.where(row_numbers == strong_rows[3], strengths[3], boost)
    values = values * boost[:, None]
    return values.astype(jnp.bfloat16)


def group_ids(group_key):
    blocks = VOCAB // V_DEV
    bound = 2 * TOK_DEV // blocks
    slots = bound * blocks
    full_block = jax.random.randint(jax.random.fold_in(group_key, 1), (), 0, blocks)
    priority = jax.random.permutation(jax.random.fold_in(group_key, 2), slots).astype(jnp.int32)
    slot_block = jnp.arange(slots, dtype=jnp.int32) // bound
    priority = jnp.where(slot_block == full_block, -1, priority)
    chosen = jnp.argsort(priority, stable=True)[:TOK_DEV].astype(jnp.int32) // bound
    shuffled = jax.random.permutation(jax.random.fold_in(group_key, 3), chosen)
    offsets = jax.random.randint(jax.random.fold_in(group_key, 4), (TOK_DEV,), 0, V_DEV)
    return (shuffled * V_DEV + offsets).astype(jnp.int32)


def draw_token_ids(key, part):
    group_count = TOKENS // TOK_DEV
    numbers = jnp.arange(group_count, dtype=jnp.int32)
    keys = jax.vmap(lambda number: jax.random.fold_in(key, 31 + number))(numbers)
    return jax.vmap(group_ids)(keys).reshape(TOKENS)


def plant(result, stream_key, smallest, high):
    longest = result.shape.index(max(result.shape))
    spots = []
    for shift in (0, 1):
        where = [jax.random.randint(jax.random.fold_in(stream_key, axis), (), 0, length) for axis, length in enumerate(result.shape)]
        where[longest] = (where[longest] + shift) % result.shape[longest]
        spots.append(tuple(where))
    return result.at[spots[0]].set(smallest).at[spots[1]].set(high)


def levels(key, shape, split, least, top_value):
    gain, own = 1.0, jax.random.fold_in(key, 6)
    for position, blocks in split:
        heights = jnp.exp(jax.random.uniform(jax.random.fold_in(own, position), (blocks,), jnp.float32, least / len(split), top_value / len(split)))
        gain = gain * jnp.repeat(heights, shape[position] // blocks).reshape([-1 if axis == position else 1 for axis in range(len(shape))])
    return gain


def rank_table(amount, lean):
    loads = [(1 << 20) // math.isqrt(rank ** lean) + 1 for rank in range(1, amount + 1)]
    width = 1 + sum(loads) // (1 << 30)
    return np.cumsum(np.array([max(1, weight // width) for weight in loads]))


def skewed_ids(rng, shape, amount, lean):
    table = rank_table(amount, lean)
    ticket = jax.random.randint(jax.random.fold_in(rng, 1), shape, 0, int(table[amount - 1]))
    standing = jnp.searchsorted(jnp.asarray(table, jnp.int32), ticket, side="right")
    return jax.random.permutation(jax.random.fold_in(rng, 2), amount)[standing].astype(jnp.int32)


def scatter_about(stream_key, extent, deviation, reach, split=(), held_as=jnp.bfloat16):
    gain = levels(stream_key, extent, split, -0.22, 0.18) if split else 1.0
    values = jax.random.normal(stream_key, extent, jnp.float32) * deviation * gain
    return jnp.minimum(jnp.maximum(values, -reach), reach).astype(held_as)


def setup_inputs(seed: int = 0) -> dict:
    key_of = jax.random.split(jax.random.key(seed), 6)
    return {
        "hidden": draw_hidden(jax.random.fold_in(key_of[5], 71), 0),
        "head_t": scatter_about(key_of[1], (D, VOCAB), (D // 9) ** -0.5, 0.25, ((0, 4), (1, 8))),
        "targets": plant(skewed_ids(key_of[2], (TOKENS,), VOCAB, 1), jax.random.fold_in(key_of[2], 3), 0, VOCAB - 1).astype(jnp.int32),
        "token_ids": draw_token_ids(jax.random.fold_in(key_of[5], 71), 0),
        "embed_cot": scatter_about(key_of[4], (TOKENS, D), 1.0, 6.0, ((0, 4),)),
    }


def reference(hidden, head_t, targets, token_ids, embed_cot):
    logits = jnp.dot(hidden, head_t, preferred_element_type=jnp.float32)
    row_max = jnp.max(logits, axis=1, keepdims=True)
    expo = jnp.exp(logits - row_max)
    row_sum = jnp.sum(expo, axis=1, keepdims=True)
    columns = jnp.arange(VOCAB, dtype=jnp.int32)[None, :]
    target_hot = (columns == targets[:, None]).astype(jnp.float32)
    dlogits = (expo / row_sum - target_hot).astype(jnp.bfloat16)
    head_grad = jnp.dot(hidden.T, dlogits, preferred_element_type=jnp.float32).astype(jnp.bfloat16)
    hidden_grad = jnp.dot(dlogits, head_t.T, preferred_element_type=jnp.float32).astype(jnp.bfloat16)
    id_hot = (columns == token_ids[:, None]).astype(jnp.bfloat16)
    embed_grad = jnp.dot(embed_cot.T, id_hot, preferred_element_type=jnp.float32).astype(jnp.bfloat16)
    return head_grad, embed_grad, hidden_grad
```

```python
import functools

import jax
import jax.numpy as jnp
from jax import lax
from jax.experimental import pallas as pl
from jax.experimental.pallas import tpu as pltpu
from jax.sharding import PartitionSpec as P

F32 = jnp.float32
BF16 = jnp.bfloat16
LANE = 128


def column_tiles(start, stop, body):
    full = (stop - start) // 256

    @pl.loop(0, full)
    def _(i):
        body(pl.multiple_of(start + i * 256, 128), 256)

    if (stop - start) % 256:
        body(start + full * 256, (stop - start) % 256)


def core_kernel(
    ndp, nv,
    hidden, cot, head, targets, ids,
    lh_out, lc_out, dl_out, ids_out, hg_out,
    w, lh, lc, idall, part, got, relay, dl, stat, srow, sall, hgp, hgs, hgd, hgr,
    loc, fs, fr, ss, sr, hs, hr, gs, gr,
):
    tok = hidden.shape[0]
    half = tok // 2
    wide, vdev = head.shape
    cut = (vdev // LANE + 1) // 2 * LANE
    rows = hg_out.shape[0]
    pairs = nv // (2 * ndp)
    chips = nv // 2
    me = lax.axis_index("dp")
    vi = lax.axis_index("vocab")
    core = lax.rem(vi, 2)
    chip = lax.div(vi, 2)
    sib = vi + 1 - 2 * core
    px = me + 1 - 2 * lax.rem(me, 2)
    py = lax.rem(me + 2, 4)
    pd = 3 - me

    def send(src, dst, ssem, rsem, dp, vocab):
        return pltpu.make_async_remote_copy(
            src_ref=src, dst_ref=dst, send_sem=ssem, recv_sem=rsem,
            device_id={"dp": dp, "vocab": vocab}, device_id_type=pl.DeviceIdType.MESH,
        )

    load_w = pltpu.make_async_copy(head, w, loc.at[0])
    load_w.start()
    load_h = pltpu.make_async_copy(
        hidden.at[:, pl.ds(pl.multiple_of(me * wide, LANE), wide)], lh.at[me], loc.at[1])
    load_h.start()
    load_c = pltpu.make_async_copy(
        cot.at[:, pl.ds(pl.multiple_of(me * wide, LANE), wide)], lc.at[me], loc.at[2])
    load_c.start()
    load_i = pltpu.make_async_copy(ids, idall.at[me], loc.at[3])
    load_i.start()

    barrier = pltpu.get_barrier_semaphore()
    for p in (px, py, pd):
        pl.semaphore_signal(barrier, inc=1, device_id={"dp": p, "vocab": vi},
                            device_id_type=pl.DeviceIdType.MESH)
    for o in range(1, nv):
        pl.semaphore_signal(barrier, inc=1, device_id={"dp": me, "vocab": lax.rem(vi + o, nv)},
                            device_id_type=pl.DeviceIdType.MESH)
    pl.semaphore_wait(barrier, ndp - 1 + nv - 1)

    mine = pl.ds(pl.multiple_of(core * half, 16), half)
    peers = (pd, px, py)

    def scatter(src, buf, base):
        out = []
        for k, p in enumerate(peers):
            c = send(src.at[mine, pl.ds(pl.multiple_of(p * wide, LANE), wide)],
                     buf.at[me, mine, :], fs.at[base + k], fr.at[base + k], p, vi)
            c.start()
            out.append(c)
        return out

    def share(buf, base, k):
        c = send(buf.at[peers[k], mine, :], buf.at[peers[k], mine, :],
                 fs.at[base + k], fr.at[base + k], me, sib)
        c.start()
        return c

    first = scatter(hidden, lh, 0)
    pending = list(first)
    load_w.wait()
    load_h.wait()

    def logits(slot, group, start, stop):
        def body(c, n):
            part[slot, :, pl.ds(c, n)] = jnp.dot(
                lh[group], w[:, pl.ds(c, n)], preferred_element_type=F32)
        column_tiles(start, stop, body)

    shared = []
    logits(0, me, 0, vdev)
    for k in range(3):
        first[k].wait_recv()
        shared.append(share(lh, 3, k))
    shared[0].wait_recv()
    lo, hi = pl.ds(0, cut), pl.ds(cut, vdev - cut)
    logits(3, pd, 0, cut)
    d_a = send(part.at[3, :, lo], relay.at[:, lo], fs.at[6], fr.at[6], px, vi)
    d_a.start()
    logits(3, pd, cut, vdev)
    d_b = send(part.at[3, :, hi], relay.at[:, hi], fs.at[7], fr.at[7], py, vi)
    d_b.start()
    shared[1].wait_recv()
    logits(1, px, 0, cut)
    x_a = send(part.at[1, :, lo], got.at[0, :, lo], fs.at[8], fr.at[8], px, vi)
    x_a.start()
    shared[2].wait_recv()
    logits(2, py, cut, vdev)
    y_b = send(part.at[2, :, hi], got.at[1, :, hi], fs.at[9], fr.at[9], py, vi)
    y_b.start()
    logits(1, px, cut, vdev)
    logits(2, py, 0, cut)

    out_lh = pltpu.make_async_copy(lh, lh_out, loc.at[1])
    out_lh.start()

    d_a.wait_recv()

    @pl.loop(0, tok // 16)
    def _(i):
        r = pl.ds(pl.multiple_of(i * 16, 16), 16)
        part[2, r, lo] = part[2, r, lo] + relay[r, lo]

    y_a = send(part.at[2, :, lo], got.at[1, :, lo], fs.at[10], fr.at[10], py, vi)
    y_a.start()
    d_b.wait_recv()

    @pl.loop(0, tok // 16)
    def _(i):
        r = pl.ds(pl.multiple_of(i * 16, 16), 16)
        part[1, r, hi] = part[1, r, hi] + relay[r, hi]

    x_b = send(part.at[1, :, hi], got.at[0, :, hi], fs.at[11], fr.at[11], px, vi)
    x_b.start()
    pending += shared + [d_a, d_b, x_a, y_b, y_a, x_b]
    for c in (x_a, y_b, y_a, x_b):
        c.wait_recv()

    load_c.wait()
    load_i.wait()
    moved = scatter(cot, lc, 12)
    pending += moved
    id_moves = []
    for k, p in enumerate(peers):
        c = send(ids, idall.at[me], fs.at[18 + k], fr.at[18 + k], p, vi)
        c.start()
        id_moves.append(c)
    pending += id_moves

    lane = lax.broadcasted_iota(jnp.int32, (16, LANE), 1)

    @pl.loop(0, tok // 16)
    def _(i):
        r = pl.ds(pl.multiple_of(i * 16, 16), 16)
        l = part[0, r, :] + got[0, r, :] + got[1, r, :]
        part[0, r, :] = l
        m = jnp.max(l, axis=1, keepdims=True)
        s = jnp.sum(jnp.exp(l - m), axis=1, keepdims=True)
        stat[r, :] = jnp.where(lane == 0, m, s)

    srow[...] = stat[...].T[:8]
    stats = []
    for o in range(1, nv):
        c = send(srow, sall.at[o], ss.at[o], sr.at[o], me, lax.rem(vi + o, nv))
        c.start()
        stats.append(c)
    sall[0] = srow[...]
    for c in stats:
        c.wait_recv()
    top = sall[0, 0:1, :]
    for o in range(1, nv):
        top = jnp.maximum(top, sall[o, 0:1, :])
    total = jnp.zeros_like(top)
    for o in range(nv):
        total = total + sall[o, 1:2, :] * jnp.exp(sall[o, 0:1, :] - top)
    sub = lax.broadcasted_iota(jnp.int32, (LANE, tok), 0)
    stat[...] = jnp.where(sub == 0, top, total).T
    for c in stats:
        c.wait_send()

    shift = vi * vdev

    @pl.loop(0, tok // 16)
    def _(i):
        r = pl.ds(pl.multiple_of(i * 16, 16), 16)
        m = stat[r, 0:1]
        s = stat[r, 1:2]
        cols = lax.broadcasted_iota(jnp.int32, (16, vdev), 1) + shift
        hot = (cols == targets[r, :]).astype(F32)
        dl[me, r, :] = (jnp.exp(part[0, r, :] - m) / s - hot).astype(BF16)

    g_x = send(dl.at[me], dl.at[me], fs.at[21], fr.at[21], px, vi)
    g_y = send(dl.at[me], dl.at[me], fs.at[22], fr.at[22], py, vi)
    g_x.start()
    g_y.start()
    pending += [g_x, g_y]

    hg_sends = []

    def hidden_grad(step, g):
        def body(c, n):
            hgp[step, :, pl.ds(c, n)] = lax.dot_general(
                dl[g], w[pl.ds(c, n), :], (((1,), (1,)), ((), ())),
                preferred_element_type=F32).astype(BF16)
        column_tiles(0, wide, body)
        out = []
        for i in range(pairs):
            away = pl.ds(pl.multiple_of((2 * i + 1 - core) * rows, 16), rows)
            c = send(hgp.at[step, away, :], hgs.at[step, i],
                     hs.at[step * pairs + i], hr.at[step * pairs + i], me, sib)
            c.start()
            out.append(c)
        return out

    def forward(step, g, out):
        for i in range(pairs):
            out[i].wait_recv()
            keep = pl.ds(pl.multiple_of((2 * i + core) * rows, 16), rows)
            hgd[step, i] = (hgp[step, keep, :].astype(F32) + hgs[step, i].astype(F32)).astype(BF16)
            dest = g * pairs + i
            slot = lax.rem(chip - dest + chips, chips)

            @pl.when(slot != 0)
            def _():
                send(hgd.at[step, i], hgr.at[slot], gs.at[step * pairs + i], gr.at[slot],
                     me, 2 * dest + core).start()

            @pl.when(slot == 0)
            def _():
                hgr[0] = hgd[step, i]

            hg_sends.append((step, i, slot, dest))

    s0 = hidden_grad(0, me)
    a, b = pl.ds(0, half), pl.ds(half, half)
    g_x.wait_recv()
    r_x = send(dl.at[px, a, :], dl.at[px, a, :], fs.at[23], fr.at[23], py, vi)
    r_x.start()
    g_y.wait_recv()
    r_y = send(dl.at[py, b, :], dl.at[py, b, :], fs.at[24], fr.at[24], px, vi)
    r_y.start()
    pending += [r_x, r_y]
    forward(0, me, s0)
    s1 = hidden_grad(1, px)
    for k in range(3):
        moved[k].wait_recv()
        c = share(lc, 15, k)
        pending.append(c)
        shared.append(c)
    forward(1, px, s1)
    s2 = hidden_grad(2, py)
    forward(2, py, s2)
    for c in shared[3:]:
        c.wait_recv()
    for c in id_moves:
        c.wait_recv()
    out_lc = pltpu.make_async_copy(lc, lc_out, loc.at[2])
    out_lc.start()
    out_id = pltpu.make_async_copy(idall, ids_out, loc.at[3])
    out_id.start()
    r_x.wait_recv()
    r_y.wait_recv()
    out_dl = pltpu.make_async_copy(dl, dl_out, loc.at[0])
    out_dl.start()
    s3 = hidden_grad(3, pd)
    forward(3, pd, s3)

    for o in range(1, chips):
        send(hgd.at[0, 0], hgr.at[o], gs.at[0], gr.at[o], me, sib).wait_recv()
    acc = hgr[0].astype(F32)
    for o in range(1, chips):
        acc = acc + hgr[o].astype(F32)
    hg_out[...] = acc.astype(BF16)

    for step, i, slot, dest in hg_sends:
        @pl.when(slot != 0)
        def _():
            send(hgd.at[step, i], hgr.at[slot], gs.at[step * pairs + i], gr.at[slot],
                 me, 2 * dest + core).wait_send()
    for c in s0 + s1 + s2 + s3 + pending:
        c.wait_send()
    for c in (out_lh, out_lc, out_id, out_dl):
        c.wait()


def core_call(ndp, nv, hidden, cot, head, targets, ids):
    tok, full = hidden.shape
    wide, vdev = head.shape
    rows = tok * ndp // nv
    pairs = nv // (2 * ndp)
    dma = pltpu.SemaphoreType.DMA
    anyspec = pl.BlockSpec(memory_space=pl.ANY)
    vspec = pl.BlockSpec(memory_space=pltpu.VMEM)
    return pl.pallas_call(
        functools.partial(core_kernel, ndp, nv),
        out_shape=(
            jax.ShapeDtypeStruct((ndp, tok, wide), BF16),
            jax.ShapeDtypeStruct((ndp, tok, wide), BF16),
            jax.ShapeDtypeStruct((ndp, tok, vdev), BF16),
            jax.ShapeDtypeStruct((ndp, 8, tok), jnp.int32),
            jax.ShapeDtypeStruct((rows, wide), BF16),
        ),
        in_specs=[anyspec, anyspec, anyspec, vspec, anyspec],
        out_specs=(anyspec, anyspec, anyspec, anyspec, vspec),
        scratch_shapes=[
            pltpu.VMEM((wide, vdev), BF16),
            pltpu.VMEM((ndp, tok, wide), BF16),
            pltpu.VMEM((ndp, tok, wide), BF16),
            pltpu.VMEM((ndp, 8, tok), jnp.int32),
            pltpu.VMEM((4, tok, vdev), F32),
            pltpu.VMEM((2, tok, vdev), F32),
            pltpu.VMEM((tok, vdev), F32),
            pltpu.VMEM((ndp, tok, vdev), BF16),
            pltpu.VMEM((tok, LANE), F32),
            pltpu.VMEM((8, tok), F32),
            pltpu.VMEM((nv, 8, tok), F32),
            pltpu.VMEM((4, tok, wide), BF16),
            pltpu.VMEM((4, pairs, rows, wide), BF16),
            pltpu.VMEM((4, pairs, rows, wide), BF16),
            pltpu.VMEM((nv // 2, rows, wide), BF16),
            dma((4,)), dma((25,)), dma((25,)), dma((nv,)), dma((nv,)),
            dma((4 * pairs,)), dma((4 * pairs,)), dma((4 * pairs,)), dma((nv // 2,)),
        ],
        compiler_params=pltpu.CompilerParams(
            collective_id=0, has_side_effects=True, vmem_limit_bytes=64000000),
        name="core",
    )(hidden, cot, head, targets, ids)


def grad_kernel(a_ref, b_ref, o_ref):
    o_ref[...] = lax.dot_general(
        a_ref[...], b_ref[...], (((0,), (0,)), ((), ())),
        preferred_element_type=F32).astype(BF16)


def head_grad_call(lh, dl):
    n, wide = lh.shape
    vdev = dl.shape[1]
    return pl.pallas_call(
        grad_kernel,
        grid=(wide // 256,),
        out_shape=jax.ShapeDtypeStruct((wide, vdev), BF16),
        in_specs=[pl.BlockSpec((n, 256), lambda i: (0, i)),
                  pl.BlockSpec((n, vdev), lambda i: (0, 0))],
        out_specs=pl.BlockSpec((256, vdev), lambda i: (i, 0)),
        name="head_grad",
    )(lh, dl)


def embed_kernel(vdev, a_ref, id_ref, o_ref, hot):
    @pl.when(pl.program_id(0) == 0)
    def _():
        shift = lax.axis_index("vocab") * vdev

        @pl.loop(0, hot.shape[0] // 16)
        def _(i):
            r = pl.ds(pl.multiple_of(i * 16, 16), 16)
            cols = lax.broadcasted_iota(jnp.int32, (16, vdev), 1) + shift
            hot[r, :] = (cols == id_ref[r, :]).astype(F32).astype(BF16)

    grad_kernel(a_ref, hot, o_ref)


def embed_grad_call(lc, ids, vdev):
    n, wide = lc.shape
    return pl.pallas_call(
        functools.partial(embed_kernel, vdev),
        grid=(wide // 256,),
        out_shape=jax.ShapeDtypeStruct((wide, vdev), BF16),
        in_specs=[pl.BlockSpec((n, 256), lambda i: (0, i)),
                  pl.BlockSpec((n, 1), lambda i: (0, 0))],
        out_specs=pl.BlockSpec((256, vdev), lambda i: (i, 0)),
        scratch_shapes=[pltpu.VMEM((n, vdev), BF16)],
        name="embed_grad",
    )(lc, ids)


def on_device(ndp, nv, hidden, head_t, targets, token_ids, embed_cot):
    tok = hidden.shape[0]
    wide, vdev = head_t.shape
    ids8 = jnp.broadcast_to(token_ids[None, :], (8, tok))
    lh, lc, dl, ids, hidden_grad = core_call(
        ndp, nv, hidden, embed_cot, head_t, targets[:, None], ids8)
    n = ndp * tok
    head_grad = head_grad_call(lh.reshape(n, wide), dl.reshape(n, vdev))
    embed_grad = embed_grad_call(lc.reshape(n, wide), ids[:, 0, :].reshape(n, 1), vdev)
    return head_grad, embed_grad, hidden_grad


def solution(mesh):
    placed = (P("dp", None), P("dp", "vocab"), P("dp"), P("dp"), P("dp", None))
    return jax.shard_map(
        functools.partial(on_device, mesh.shape["dp"], mesh.shape["vocab"]),
        mesh=mesh,
        in_specs=placed,
        out_specs=(P("dp", "vocab"), P("dp", "vocab"), P("vocab", "dp")),
        check_vma=False,
    )
```

```python
import functools

import jax
import jax.numpy as jnp
from jax import lax
from jax.experimental import pallas as pl
from jax.experimental.pallas import tpu as pltpu
from jax.sharding import PartitionSpec as P

F32 = jnp.float32
BF16 = jnp.bfloat16
LANE = 128


def column_tiles(start, stop, body):
    full = (stop - start) // 256

    @pl.loop(0, full)
    def _(i):
        body(pl.multiple_of(start + i * 256, 128), 256)

    if (stop - start) % 256:
        body(start + full * 256, (stop - start) % 256)


def core_kernel(
    ndp, nv,
    hidden, cot, head, targets, ids,
    lh_out, lc_out, dl_out, ids_out, hg_out,
    w, lh, cotv, sel, pick, lc, idsend, idall, tcol, part, got, relay, dl, stat, srow, sall, hgp, hgs, hgd, hgr,
    loc, fs, fr, ss, sr, hs, hr, gs, gr,
):
    tok = hidden.shape[0]
    half = tok // 2
    wide, vdev = head.shape
    cut = (vdev // LANE + 1) // 2 * LANE
    rows = hg_out.shape[0]
    bound = lc.shape[1]
    quarter = tok // 4
    pairs = nv // (2 * ndp)
    chips = nv // 2
    me = lax.axis_index("dp")
    vi = lax.axis_index("vocab")
    core = lax.rem(vi, 2)
    chip = lax.div(vi, 2)
    sib = vi + 1 - 2 * core
    odd = lax.rem(chip, 2)
    zp = vi + 2 - 4 * odd
    px = me + 1 - 2 * lax.rem(me, 2)
    py = lax.rem(me + 2, 4)
    pd = 3 - me

    def send(src, dst, ssem, rsem, dp, vocab):
        return pltpu.make_async_remote_copy(
            src_ref=src, dst_ref=dst, send_sem=ssem, recv_sem=rsem,
            device_id={"dp": dp, "vocab": vocab}, device_id_type=pl.DeviceIdType.MESH,
        )

    load_w = pltpu.make_async_copy(head, w, loc.at[0])
    load_w.start()
    load_h = pltpu.make_async_copy(
        hidden.at[:, pl.ds(pl.multiple_of(me * wide, LANE), wide)], lh.at[me], loc.at[1])
    load_h.start()
    load_c = pltpu.make_async_copy(cot, cotv, loc.at[2])
    load_c.start()

    barrier = pltpu.get_barrier_semaphore()
    for p in (px, py, pd):
        pl.semaphore_signal(barrier, inc=1, device_id={"dp": p, "vocab": vi},
                            device_id_type=pl.DeviceIdType.MESH)
    for o in range(1, nv):
        pl.semaphore_signal(barrier, inc=1, device_id={"dp": me, "vocab": lax.rem(vi + o, nv)},
                            device_id_type=pl.DeviceIdType.MESH)
    pl.semaphore_wait(barrier, ndp - 1 + nv - 1)

    mine = pl.ds(pl.multiple_of((2 * odd + core) * quarter, 16), quarter)
    theirs = pl.ds(pl.multiple_of((2 - 2 * odd + core) * quarter, 16), quarter)
    peers = (pd, px, py)

    first = []
    for k, p in enumerate(peers):
        c = send(hidden.at[mine, pl.ds(pl.multiple_of(p * wide, LANE), wide)],
                 lh.at[me, mine, :], fs.at[k], fr.at[k], p, vi)
        c.start()
        first.append(c)
    pending = list(first)

    def share(k):
        out = []
        first[k].wait_recv()
        for dst, n in ((zp, 0), (sib, 1)):
            c = send(lh.at[peers[k], mine, :], lh.at[peers[k], mine, :],
                     fs.at[3 + 3 * k + n], fr.at[3 + 3 * k + n], me, dst)
            c.start()
            out.append(c)
        return out

    def relay_on(k, out):
        out[0].wait_recv()
        c = send(lh.at[peers[k], theirs, :], lh.at[peers[k], theirs, :],
                 fs.at[5 + 3 * k], fr.at[5 + 3 * k], me, sib)
        c.start()
        out.append(c)

    load_w.wait()
    load_h.wait()

    def logits(slot, group, start, stop):
        def body(c, n):
            part[slot, :, pl.ds(c, n)] = jnp.dot(
                lh[group], w[:, pl.ds(c, n)], preferred_element_type=F32)
        column_tiles(start, stop, body)

    logits(0, me, 0, cut)
    shared = [share(0), share(1), share(2)]
    logits(0, me, cut, vdev)
    for k in range(3):
        relay_on(k, shared[k])

    def arrived(k):
        shared[k][1].wait_recv()
        shared[k][2].wait_recv()

    arrived(0)
    lo, hi = pl.ds(0, cut), pl.ds(cut, vdev - cut)
    logits(3, pd, 0, cut)
    d_a = send(part.at[3, :, lo], relay.at[:, lo], fs.at[12], fr.at[12], px, vi)
    d_a.start()
    logits(3, pd, cut, vdev)
    d_b = send(part.at[3, :, hi], relay.at[:, hi], fs.at[13], fr.at[13], py, vi)
    d_b.start()
    arrived(1)
    logits(1, px, 0, cut)
    x_a = send(part.at[1, :, lo], got.at[0, :, lo], fs.at[14], fr.at[14], px, vi)
    x_a.start()
    arrived(2)
    logits(2, py, cut, vdev)
    y_b = send(part.at[2, :, hi], got.at[1, :, hi], fs.at[15], fr.at[15], py, vi)
    y_b.start()
    logits(1, px, cut, vdev)
    logits(2, py, 0, cut)

    out_lh = pltpu.make_async_copy(lh, lh_out, loc.at[1])
    out_lh.start()

    tcol[...] = jnp.broadcast_to(targets[...].astype(F32), (LANE, tok)).T
    place = jnp.broadcast_to(ids[...].astype(F32), (LANE, tok)).T - (vi * vdev).astype(F32)
    inside = jnp.logical_and(place >= 0, place < vdev)
    before = (lax.broadcasted_iota(jnp.int32, (tok, tok), 0)
              > lax.broadcasted_iota(jnp.int32, (tok, tok), 1)).astype(F32).astype(BF16)
    rank = jnp.dot(before, inside.astype(F32).astype(BF16), preferred_element_type=F32)
    slot_no = lax.broadcasted_iota(jnp.int32, (tok, LANE), 1).astype(F32)
    sel[...] = jnp.logical_and(rank == slot_no, inside).astype(F32).astype(BF16)
    mark = jnp.where(inside, place + 1, 0.0)
    high = jnp.floor(mark / 64)
    low = mark - 64 * high

    def squeeze(x):
        return lax.dot_general(sel[...], x, (((0,), (0,)), ((), ())),
                               preferred_element_type=F32)[:bound]

    idsend[...] = 64 * squeeze(high.astype(BF16)) + squeeze(low.astype(BF16)) - 1
    load_c.wait()

    def compact(c, n):
        pick[:, pl.ds(c, n)] = squeeze(cotv[:, pl.ds(c, n)]).astype(BF16)

    column_tiles(0, ndp * wide, compact)
    load_p = pltpu.make_async_copy(
        pick.at[:, pl.ds(pl.multiple_of(me * wide, LANE), wide)], lc.at[me], loc.at[2])
    load_p.start()
    load_i = pltpu.make_async_copy(idsend, idall.at[me], loc.at[3])
    load_i.start()

    d_a.wait_recv()

    @pl.loop(0, tok // 16)
    def _(i):
        r = pl.ds(pl.multiple_of(i * 16, 16), 16)
        part[2, r, lo] = part[2, r, lo] + relay[r, lo]

    y_a = send(part.at[2, :, lo], got.at[1, :, lo], fs.at[16], fr.at[16], py, vi)
    y_a.start()
    d_b.wait_recv()

    @pl.loop(0, tok // 16)
    def _(i):
        r = pl.ds(pl.multiple_of(i * 16, 16), 16)
        part[1, r, hi] = part[1, r, hi] + relay[r, hi]

    x_b = send(part.at[1, :, hi], got.at[0, :, hi], fs.at[17], fr.at[17], px, vi)
    x_b.start()
    pending += shared[0] + shared[1] + shared[2] + [d_a, d_b, x_a, y_b, y_a, x_b]
    for c in (x_a, y_b, y_a, x_b):
        c.wait_recv()

    load_p.wait()
    load_i.wait()
    moved = []
    for k, p in enumerate(peers):
        c = send(pick.at[:, pl.ds(pl.multiple_of(p * wide, LANE), wide)], lc.at[me],
                 fs.at[18 + k], fr.at[18 + k], p, vi)
        c.start()
        moved.append(c)
        c = send(idsend, idall.at[me], fs.at[21 + k], fr.at[21 + k], p, vi)
        c.start()
        moved.append(c)
    pending += moved

    lane = lax.broadcasted_iota(jnp.int32, (16, LANE), 1)

    @pl.loop(0, tok // 16)
    def _(i):
        r = pl.ds(pl.multiple_of(i * 16, 16), 16)
        l = part[0, r, :] + got[0, r, :] + got[1, r, :]
        part[0, r, :] = l
        m = jnp.max(l, axis=1, keepdims=True)
        s = jnp.sum(jnp.exp(l - m), axis=1, keepdims=True)
        stat[r, :] = jnp.where(lane == 0, m, s)

    srow[...] = stat[...].T[:8]
    stats = []
    for o in range(1, nv):
        c = send(srow, sall.at[o], ss.at[o], sr.at[o], me, lax.rem(vi + o, nv))
        c.start()
        stats.append(c)
    sall[0] = srow[...]
    for c in stats:
        c.wait_recv()
    top = sall[0, 0:1, :]
    for o in range(1, nv):
        top = jnp.maximum(top, sall[o, 0:1, :])
    total = jnp.zeros_like(top)
    for o in range(nv):
        total = total + sall[o, 1:2, :] * jnp.exp(sall[o, 0:1, :] - top)
    sub = lax.broadcasted_iota(jnp.int32, (LANE, tok), 0)
    stat[...] = jnp.where(sub == 0, top, total).T
    for c in stats:
        c.wait_send()

    shift = vi * vdev

    @pl.loop(0, tok // 16)
    def _(i):
        r = pl.ds(pl.multiple_of(i * 16, 16), 16)
        m = stat[r, 0:1]
        s = stat[r, 1:2]
        cols = lax.broadcasted_iota(jnp.int32, (16, vdev), 1) + shift
        hot = (cols == tcol[r, 0:1].astype(jnp.int32)).astype(F32)
        dl[me, r, :] = (jnp.exp(part[0, r, :] - m) / s - hot).astype(BF16)

    g_x = send(dl.at[me], dl.at[me], fs.at[24], fr.at[24], px, vi)
    g_y = send(dl.at[me], dl.at[me], fs.at[25], fr.at[25], py, vi)
    g_x.start()
    g_y.start()
    pending += [g_x, g_y]

    hg_sends = []

    def hidden_grad(step, g):
        def body(c, n):
            hgp[step, :, pl.ds(c, n)] = lax.dot_general(
                dl[g], w[pl.ds(c, n), :], (((1,), (1,)), ((), ())),
                preferred_element_type=F32)
        column_tiles(0, wide, body)
        out = []
        for i in range(pairs):
            away = pl.ds(pl.multiple_of((2 * i + 1 - core) * rows, 16), rows)
            c = send(hgp.at[step, away, :], hgs.at[step, i],
                     hs.at[step * pairs + i], hr.at[step * pairs + i], me, sib)
            c.start()
            out.append(c)
        return out

    def forward(step, g, out):
        for i in range(pairs):
            out[i].wait_recv()
            keep = pl.ds(pl.multiple_of((2 * i + core) * rows, 16), rows)
            hgd[step, i] = (hgp[step, keep, :] + hgs[step, i]).astype(BF16)
            dest = g * pairs + i
            slot = lax.rem(chip - dest + chips, chips)

            @pl.when(slot != 0)
            def _():
                send(hgd.at[step, i], hgr.at[slot], gs.at[step * pairs + i], gr.at[slot],
                     me, 2 * dest + core).start()

            @pl.when(slot == 0)
            def _():
                hgr[0] = hgd[step, i]

            hg_sends.append((step, i, slot, dest))

    s0 = hidden_grad(0, me)
    a, b = pl.ds(0, half), pl.ds(half, half)
    g_x.wait_recv()
    r_x = send(dl.at[px, a, :], dl.at[px, a, :], fs.at[26], fr.at[26], py, vi)
    r_x.start()
    g_y.wait_recv()
    r_y = send(dl.at[py, b, :], dl.at[py, b, :], fs.at[27], fr.at[27], px, vi)
    r_y.start()
    pending += [r_x, r_y]
    forward(0, me, s0)
    s1 = hidden_grad(1, px)
    forward(1, px, s1)
    s2 = hidden_grad(2, py)
    forward(2, py, s2)
    for c in moved:
        c.wait_recv()
    out_lc = pltpu.make_async_copy(lc, lc_out, loc.at[2])
    out_lc.start()
    out_id = pltpu.make_async_copy(idall, ids_out, loc.at[3])
    out_id.start()
    r_x.wait_recv()
    r_y.wait_recv()
    out_dl = pltpu.make_async_copy(dl, dl_out, loc.at[0])
    out_dl.start()
    s3 = hidden_grad(3, pd)
    forward(3, pd, s3)

    for o in range(1, chips):
        send(hgd.at[0, 0], hgr.at[o], gs.at[0], gr.at[o], me, sib).wait_recv()
    acc = hgr[0].astype(F32)
    for o in range(1, chips):
        acc = acc + hgr[o].astype(F32)
    hg_out[...] = acc.astype(BF16)

    for step, i, slot, dest in hg_sends:
        @pl.when(slot != 0)
        def _():
            send(hgd.at[step, i], hgr.at[slot], gs.at[step * pairs + i], gr.at[slot],
                 me, 2 * dest + core).wait_send()
    for c in s0 + s1 + s2 + s3 + pending:
        c.wait_send()
    for c in (out_lh, out_lc, out_id, out_dl):
        c.wait()


def core_call(ndp, nv, hidden, cot, head, targets, ids):
    tok, full = hidden.shape
    wide, vdev = head.shape
    rows = tok * ndp // nv
    pairs = nv // (2 * ndp)
    bound = 2 * tok // nv
    dma = pltpu.SemaphoreType.DMA
    anyspec = pl.BlockSpec(memory_space=pl.ANY)
    vspec = pl.BlockSpec(memory_space=pltpu.VMEM)
    return pl.pallas_call(
        functools.partial(core_kernel, ndp, nv),
        out_shape=(
            jax.ShapeDtypeStruct((ndp, tok, wide), BF16),
            jax.ShapeDtypeStruct((ndp, bound, wide), BF16),
            jax.ShapeDtypeStruct((ndp, tok, vdev), BF16),
            jax.ShapeDtypeStruct((ndp, bound, LANE), F32),
            jax.ShapeDtypeStruct((rows, wide), BF16),
        ),
        in_specs=[anyspec, anyspec, anyspec, vspec, vspec],
        out_specs=(anyspec, anyspec, anyspec, anyspec, vspec),
        scratch_shapes=[
            pltpu.VMEM((wide, vdev), BF16),
            pltpu.VMEM((ndp, tok, wide), BF16),
            pltpu.VMEM((tok, full), BF16),
            pltpu.VMEM((tok, LANE), BF16),
            pltpu.VMEM((bound, full), BF16),
            pltpu.VMEM((ndp, bound, wide), BF16),
            pltpu.VMEM((bound, LANE), F32),
            pltpu.VMEM((ndp, bound, LANE), F32),
            pltpu.VMEM((tok, LANE), F32),
            pltpu.VMEM((4, tok, vdev), F32),
            pltpu.VMEM((2, tok, vdev), F32),
            pltpu.VMEM((tok, vdev), F32),
            pltpu.VMEM((ndp, tok, vdev), BF16),
            pltpu.VMEM((tok, LANE), F32),
            pltpu.VMEM((8, tok), F32),
            pltpu.VMEM((nv, 8, tok), F32),
            pltpu.VMEM((4, tok, wide), F32),
            pltpu.VMEM((4, pairs, rows, wide), F32),
            pltpu.VMEM((4, pairs, rows, wide), BF16),
            pltpu.VMEM((nv // 2, rows, wide), BF16),
            dma((4,)), dma((28,)), dma((28,)), dma((nv,)), dma((nv,)),
            dma((4 * pairs,)), dma((4 * pairs,)), dma((4 * pairs,)), dma((nv // 2,)),
        ],
        compiler_params=pltpu.CompilerParams(
            collective_id=0, has_side_effects=True, vmem_limit_bytes=64000000),
        name="core",
    )(hidden, cot, head, targets, ids)


def grad_kernel(a_ref, b_ref, o_ref):
    o_ref[...] = lax.dot_general(
        a_ref[...], b_ref[...], (((0,), (0,)), ((), ())),
        preferred_element_type=F32).astype(BF16)


def head_grad_call(lh, dl):
    n, wide = lh.shape
    vdev = dl.shape[1]
    return pl.pallas_call(
        grad_kernel,
        grid=(wide // 256,),
        out_shape=jax.ShapeDtypeStruct((wide, vdev), BF16),
        in_specs=[pl.BlockSpec((n, 256), lambda i: (0, i)),
                  pl.BlockSpec((n, vdev), lambda i: (0, 0))],
        out_specs=pl.BlockSpec((256, vdev), lambda i: (i, 0)),
        name="head_grad",
    )(lh, dl)


def embed_kernel(vdev, a_ref, id_ref, o_ref, hot):
    @pl.when(pl.program_id(0) == 0)
    def _():
        @pl.loop(0, hot.shape[0] // 16)
        def _(i):
            r = pl.ds(pl.multiple_of(i * 16, 16), 16)
            cols = lax.broadcasted_iota(jnp.int32, (16, vdev), 1)
            hot[r, :] = (cols == id_ref[r, 0:1].astype(jnp.int32)).astype(F32).astype(BF16)

    grad_kernel(a_ref, hot, o_ref)


def embed_grad_call(lc, ids, vdev):
    n, wide = lc.shape
    return pl.pallas_call(
        functools.partial(embed_kernel, vdev),
        grid=(wide // 256,),
        out_shape=jax.ShapeDtypeStruct((wide, vdev), BF16),
        in_specs=[pl.BlockSpec((n, 256), lambda i: (0, i)),
                  pl.BlockSpec((n, LANE), lambda i: (0, 0))],
        out_specs=pl.BlockSpec((256, vdev), lambda i: (i, 0)),
        scratch_shapes=[pltpu.VMEM((n, vdev), BF16)],
        name="embed_grad",
    )(lc, ids)


def on_device(ndp, nv, hidden, head_t, targets, token_ids, embed_cot):
    tok = hidden.shape[0]
    wide, vdev = head_t.shape
    lh, lc, dl, ids, hidden_grad = core_call(
        ndp, nv, hidden, embed_cot, head_t, targets[None, :], token_ids[None, :])
    n = ndp * tok
    head_grad = head_grad_call(lh.reshape(n, wide), dl.reshape(n, vdev))
    slots = lc.shape[0] * lc.shape[1]
    embed_grad = embed_grad_call(lc.reshape(slots, wide), ids.reshape(slots, LANE), vdev)
    return head_grad, embed_grad, hidden_grad


def solution(mesh):
    placed = (P("dp", None), P("dp", "vocab"), P("dp"), P("dp"), P("dp", None))
    return jax.shard_map(
        functools.partial(on_device, mesh.shape["dp"], mesh.shape["vocab"]),
        mesh=mesh,
        in_specs=placed,
        out_specs=(P("dp", "vocab"), P("dp", "vocab"), P("vocab", "dp")),
        check_vma=False,
    )
```
